32 devices in a mesh: gx: 4 (over y, core), gy: 8 (over z, x).
Axes of the slice: x: 2, y: 2, z: 4, core: 2. Of those that a mesh axis runs over, the one named last changes fastest.
Arguments:
- local_schur: float32 [4096, 8192], P('gx', 'gy'), as said below
- boundary_map: int32 [4, 8, 1024], P('gx', 'gy'), may hold values from 0 to 1023, each once within a row
- order_first: int32 [2, 8, 256], P(None, 'gy'), may hold values from 0 to 255, each once within a row
- order_second: int32 [2, 4, 512], replicated, may hold values from 0 to 511, each once within a row
Outputs:
- first_factor: float32 [512, 2048], P('gx', 'gy')
- first_panel: float32 [3072, 2048], P('gx', 'gy')
- second_factor: float32 [1024, 2048], P('gx', 'gy')
- second_panel: float32 [2048, 4096], P('gx', 'gy')
- merged_schur: float32 [2048, 16384], P('gx', 'gy')
The draws below stay inside these ranges and needn't reach their ends.
Inputs may be any that keep to these rules, and one draw needn't show every extreme that they name: `local_schur`: each 1024 x 1024 block is symmetric positive definite. `boundary_map`: the 1024 slots of a subdomain hold each of its boundary nodes once. `order_first`: each row lists the 256 nodes of one separator once each. `order_second`: each row lists the 512 nodes of one separator once each.
All inputs are finite; a program needn't handle non-finite values.
Results may differ from the reference program's by a relative error of at most 0.0001.
Values sent between devices are 32-bit elements; how exact they have to be, the bound alone decides.
A program may use at most 128 MiB of HBM per device.

```python
import jax
import jax.numpy as jnp
from jax import lax

SEP = 256
BND = 1024
SUB_ROWS = 4
SUB_COLS = 8
PAIR_ROWS = 2
PAIR_COLS = 4
ROWS_ALL = 4096
COLS_ALL = 8192


def draw_local_schur(key, part):
    sub_rows = ROWS_ALL // BND
    sub_cols = COLS_ALL // BND
    key_list = jax.random.split(jax.random.fold_in(key, 17), 3)
    grid_shape = (sub_rows, BND, sub_cols, BND)
    node_shape = (sub_rows, BND, sub_cols)
    noise_part = jax.random.uniform(key_list[0], grid_shape, jnp.float32, -1.0, 1.0)
    noise_part = 0.5 * (noise_part + jnp.transpose(noise_part, (0, 3, 2, 1)))
    spread = jax.random.uniform(key_list[1], node_shape, jnp.float32, 0.6, 1.4)
    margin = jax.random.uniform(key_list[2], node_shape, jnp.float32, 0.05, 1.0)
    row_scale = spread[:, :, :, None]
    col_scale = jnp.transpose(spread, (0, 2, 1))[:, None, :, :]
    slot_index = jnp.arange(BND, dtype=jnp.int32)
    product = (slot_index[:, None] + 1) * (slot_index[None, :] + 1) % (2 * (BND + 1))
    sine_table = jnp.sqrt(2.0 / (BND + 1.0)) * jnp.sin(jnp.pi * product.astype(jnp.float32) / (BND + 1.0))
    diagonal = (slot_index[:, None] == slot_index[None, :])[None, :, None, :]
    noise_scale = 0.3 / jnp.sqrt(jnp.float32(BND))
    matrix = 1.5 * row_scale * sine_table[None, :, None, :] * col_scale
    matrix = matrix + jnp.where(diagonal, 0.0, noise_scale * noise_part)
    matrix = matrix + jnp.where(diagonal, 3.3 * (1.0 + margin[:, :, :, None]), 0.0)
    return matrix.reshape(ROWS_ALL, COLS_ALL).astype(jnp.float32)


def setup_inputs(seed: int = 0) -> dict:
    seeds = jax.random.split(jax.random.key(seed), 5)
    return {
        "local_schur": draw_local_schur(jax.random.fold_in(seeds[4], 71), 0),
        "boundary_map": jax.vmap(lambda own: jax.random.permutation(own, BND))(jax.random.split(seeds[1], SUB_ROWS * SUB_COLS)).reshape((SUB_ROWS, SUB_COLS, BND)).astype(jnp.int32),
        "order_first": jax.vmap(lambda own: jax.random.permutation(own, SEP))(jax.random.split(seeds[2], PAIR_ROWS * SUB_COLS)).reshape((PAIR_ROWS, SUB_COLS, SEP)).astype(jnp.int32),
        "order_second": jax.vmap(lambda own: jax.random.permutation(own, 2 * SEP))(jax.random.split(seeds[3], PAIR_ROWS * PAIR_COLS)).reshape((PAIR_ROWS, PAIR_COLS, 2 * SEP)).astype(jnp.int32),
    }


highest = lax.Precision.HIGHEST

def reorder(sub_block, slots, left_side, upper_side):
    edge_index = slots // SEP
    west_pos = jnp.where(left_side, 1, 0).astype(jnp.int32)
    north_pos = jnp.where(upper_side, 2, 3).astype(jnp.int32)
    new_edge = jnp.where(edge_index == 0, west_pos, jnp.where(edge_index == 1, 1 - west_pos, jnp.where(edge_index == 2, north_pos, 5 - north_pos)))
    target = (new_edge * SEP + slots % SEP).astype(jnp.int32)
    inverse = jnp.zeros_like(target).at[target].set(jnp.arange(target.shape[0], dtype=jnp.int32))
    return sub_block[inverse][:, inverse]

def gram_rows(left_rows, right_rows):
    return jnp.einsum('ik,jk->ij', left_rows.astype(jnp.float32), right_rows.astype(jnp.float32), precision=highest, preferred_element_type=jnp.float32)

def panel_solve(factor, coupling):
    return lax.linalg.triangular_solve(factor, coupling, left_side=False, lower=True, transpose_a=True)

def pick_blocks(matrix, row_list, col_list):
    rows_built = []
    for row_block in row_list:
        pieces = [matrix[row_block * SEP:(row_block + 1) * SEP, col_block * SEP:(col_block + 1) * SEP] for col_block in col_list]
        rows_built.append(jnp.concatenate(pieces, axis=1))
    return jnp.concatenate(rows_built, axis=0)

def block_diagonal(upper_part, lower_part):
    zero_part = jnp.zeros_like(upper_part)
    return jnp.concatenate([jnp.concatenate([upper_part, zero_part], axis=1), jnp.concatenate([zero_part, lower_part], axis=1)], axis=0)

def first_level(upper_block, lower_block, order_one):
    inner_rows = 3 * SEP
    pivot_one = upper_block[inner_rows:, inner_rows:] + lower_block[inner_rows:, inner_rows:]
    factor_one = jnp.linalg.cholesky(pivot_one[order_one][:, order_one])
    coupling = jnp.concatenate([upper_block[:inner_rows, inner_rows:], lower_block[:inner_rows, inner_rows:]], axis=0)[:, order_one]
    panels = panel_solve(factor_one, coupling)
    placed = block_diagonal(upper_block[:inner_rows, :inner_rows], lower_block[:inner_rows, :inner_rows])
    reduced = placed - gram_rows(panels, panels)
    return (factor_one, panels, reduced)

def reference(local_schur, boundary_map, order_first, order_second):
    outputs_init = (jnp.zeros((PAIR_ROWS * SEP, SUB_COLS * SEP), jnp.float32), jnp.zeros((SUB_ROWS * 3 * SEP, SUB_COLS * SEP), jnp.float32), jnp.zeros((SUB_ROWS * SEP, SUB_COLS * SEP), jnp.float32), jnp.zeros((SUB_ROWS * 2 * SEP, SUB_COLS * 2 * SEP), jnp.float32), jnp.zeros((SUB_ROWS * 2 * SEP, SUB_COLS * 8 * SEP), jnp.float32))
    half_rows = SEP // 2

    def one_group(group_index, outputs_now):
        group_index = jnp.asarray(group_index).astype(jnp.int32)
        pair_row = (group_index // PAIR_COLS).astype(jnp.int32)
        pair_col = (group_index % PAIR_COLS).astype(jnp.int32)
        zero_index = (pair_row * 0).astype(jnp.int32)
        order_two = lax.dynamic_slice(order_second, (pair_row, pair_col, zero_index), (1, 1, 2 * SEP))[0, 0]
        first_factor, first_panel, second_factor, second_panel, merged_schur = outputs_now
        reduced_sides = []
        for col_side in range(2):
            block_col = (pair_col + col_side * PAIR_COLS).astype(jnp.int32)
            ordered = []
            for row_side in range(2):
                block_row = (pair_row + row_side * PAIR_ROWS).astype(jnp.int32)
                sub_block = lax.dynamic_slice(local_schur, (block_row * BND, block_col * BND), (BND, BND))
                slots = lax.dynamic_slice(boundary_map, (block_row, block_col, zero_index), (1, 1, BND))[0, 0]
                ordered.append(reorder(sub_block, slots, col_side == 0, row_side == 0))
            order_one = lax.dynamic_slice(order_first, (pair_row, block_col, zero_index), (1, 1, SEP))[0, 0]
            factor_one, panels, reduced = first_level(ordered[0], ordered[1], order_one)
            column = (block_col * SEP).astype(jnp.int32)
            first_factor = lax.dynamic_update_slice(first_factor, factor_one[:half_rows], (pair_row * half_rows, column))
            first_factor = lax.dynamic_update_slice(first_factor, factor_one[half_rows:], ((pair_row + PAIR_ROWS) * half_rows, column))
            first_panel = lax.dynamic_update_slice(first_panel, panels[:3 * SEP], (pair_row * (3 * SEP), column))
            first_panel = lax.dynamic_update_slice(first_panel, panels[3 * SEP:], ((pair_row + PAIR_ROWS) * (3 * SEP), column))
            reduced_sides.append(reduced)
        left_reduced, right_reduced = reduced_sides
        inner_set = [0, 3]
        outer_set = [1, 2, 4, 5]
        pivot_two = pick_blocks(left_reduced, inner_set, inner_set) + pick_blocks(right_reduced, inner_set, inner_set)
        factor_two = jnp.linalg.cholesky(pivot_two[order_two][:, order_two])
        coupling_two = jnp.concatenate([pick_blocks(left_reduced, outer_set, inner_set), pick_blocks(right_reduced, outer_set, inner_set)], axis=0)[:, order_two]
        panels_two = panel_solve(factor_two, coupling_two)
        placed_two = block_diagonal(pick_blocks(left_reduced, outer_set, outer_set), pick_blocks(right_reduced, outer_set, outer_set))
        merged = placed_two - gram_rows(panels_two, panels_two)
        for row_side in range(2):
            for col_side in range(2):
                block_row = (pair_row + row_side * PAIR_ROWS).astype(jnp.int32)
                block_col = (pair_col + col_side * PAIR_COLS).astype(jnp.int32)
                slot = 2 * col_side + row_side
                second_factor = lax.dynamic_update_slice(second_factor, factor_two[row_side * SEP:(row_side + 1) * SEP, col_side * SEP:(col_side + 1) * SEP], (block_row * SEP, block_col * SEP))
                second_panel = lax.dynamic_update_slice(second_panel, panels_two[slot * 2 * SEP:(slot + 1) * 2 * SEP], (block_row * (2 * SEP), block_col * (2 * SEP)))
                merged_schur = lax.dynamic_update_slice(merged_schur, merged[slot * 2 * SEP:(slot + 1) * 2 * SEP], (block_row * (2 * SEP), block_col * (8 * SEP)))
        return (first_factor, first_panel, second_factor, second_panel, merged_schur)
    results = lax.fori_loop(0, PAIR_ROWS * PAIR_COLS, one_group, outputs_init)
    first_factor, first_panel, second_factor, second_panel, merged_schur = results
    return (first_factor, first_panel, second_factor, second_panel, merged_schur)
```

```python
import jax
import jax.numpy as jnp
from jax import lax
from jax.experimental import pallas as pl
from jax.experimental.pallas import tpu as pltpu
from jax.sharding import PartitionSpec as P

SEP = 256

STEP = 64


def halves(x):
    high = x.astype(jnp.bfloat16)
    low = (x - high.astype(jnp.float32)).astype(jnp.bfloat16)
    return high, low


def mm(a, b, dims):
    return lax.dot_general(a, b, (dims, ((), ())), preferred_element_type=jnp.float32)


def mm3(a, b, dims):
    a_high, a_low = halves(a)
    b_high, b_low = halves(b)
    return mm(a_high, b_high, dims) + (mm(a_high, b_low, dims) + mm(a_low, b_high, dims))


def eliminate(tiles):
    count = len(tiles)
    sub = lax.broadcasted_iota(jnp.int32, (8, 128), 0)
    for t in range(count):
        cols = {
            g: [jnp.broadcast_to(tiles[g][:, 8 * t + k : 8 * t + k + 1], (8, 128)) for k in range(8)]
            for g in range(t, count)
        }
        for k in range(8):
            scale = lax.rsqrt(cols[t][k][k : k + 1, :])
            final_row = tiles[t][k : k + 1, :] * scale
            diag_row = [cols[t][m][k : k + 1, :] * scale for m in range(k + 1, 8)]
            for g in range(t, count):
                factor = cols[g][k] * scale
                if g == t:
                    factor = jnp.where(sub > k, factor, 0.0)
                for m in range(k + 1, 8):
                    cols[g][m] = cols[g][m] - factor * diag_row[m - k - 1]
                tiles[g] = tiles[g] - factor * final_row
            tiles[t] = jnp.where(sub == k, final_row, tiles[t])
    return tiles


def chol_kernel(q_ref, order_ref, lower_ref, inv_ref, work):
    n = q_ref.shape[0]
    pick = (order_ref[...] == lax.broadcasted_iota(jnp.int32, (n, n), 1)).astype(jnp.float32)
    pick16 = pick.astype(jnp.bfloat16)
    q_high, q_low = halves(q_ref[...])
    rows = mm(pick16, q_high, ((1,), (0,))) + mm(pick16, q_low, ((1,), (0,)))
    r_high, r_low = halves(rows)
    work[:, :n] = mm(r_high, pick16, ((1,), (1,))) + mm(r_low, pick16, ((1,), (1,)))
    work[:, n:] = pick
    lane = lax.broadcasted_iota(jnp.int32, (STEP, 128), 1)
    eye = jnp.where(
        lane == lax.broadcasted_iota(jnp.int32, (STEP, 128), 0) + STEP, 1.0, 0.0
    )

    def panel(p, carry):
        start = pl.multiple_of(p * STEP, STEP)
        base = pl.multiple_of((p // 2) * 128, 128)
        block = work[pl.ds(start, STEP), pl.ds(base, 128)]
        block = jnp.where(p % 2 == 0, block, pltpu.roll(block, STEP, 1))
        block = jnp.where(lane < STEP, block, eye)
        tiles = eliminate([block[8 * g : 8 * g + 8, :] for g in range(STEP // 8)])
        inverse = jnp.concatenate(tiles, axis=0)[:, STEP:]
        strip = mm3(inverse, work[pl.ds(start, STEP), :], ((1,), (0,)))
        work[pl.ds(start, STEP), :] = strip
        s_high, s_low = halves(strip)
        column = lax.broadcasted_iota(jnp.int32, (STEP, n), 1)
        after = column >= start + STEP
        c_high, c_low = halves(jnp.where(after, strip[:, :n], 0.0))
        left = jnp.concatenate([c_high, c_high, c_low, c_low], axis=0)
        right = jnp.concatenate([s_high, s_low, s_high, s_low], axis=0)
        work[...] -= mm(left, right, ((0,), (0,)))
        return carry

    lax.fori_loop(0, n // STEP, panel, 0)
    row = lax.broadcasted_iota(jnp.int32, (n, n), 0)
    col = lax.broadcasted_iota(jnp.int32, (n, n), 1)
    lower_ref[...] = jnp.where(row <= col, work[:, :n], 0.0).T
    inv_ref[...] = work[:, n:]


def chol(q, order):
    n = q.shape[0]
    spec = pl.BlockSpec(memory_space=pltpu.VMEM)
    return pl.pallas_call(
        chol_kernel,
        out_shape=(jax.ShapeDtypeStruct((n, n), jnp.float32),) * 2,
        in_specs=[spec, spec],
        out_specs=(spec, spec),
        scratch_shapes=[pltpu.VMEM((n, 2 * n), jnp.float32)],
        compiler_params=pltpu.CompilerParams(vmem_limit_bytes=40 << 20),
        cost_estimate=pl.CostEstimate(flops=n * 60_000_000, bytes_accessed=12 * n * n, transcendentals=0),
    )(q, order.reshape(n, 1))


def reorder_kernel(row_ranks, col_count, a_ref, row_ref, col_ref, out_ref):
    n = a_ref.shape[0]
    rows = lax.broadcasted_iota(jnp.int32, (SEP, n), 0)
    picked = [jnp.where(rows + rank * SEP == row_ref[...], 1.0, 0.0) for rank in row_ranks]
    pick = jnp.concatenate(picked, axis=0).astype(jnp.bfloat16)
    a_high, a_low = halves(a_ref[...])
    moved = mm(pick, a_high, ((1,), (0,))) + mm(pick, a_low, ((1,), (0,)))
    m_high, m_low = halves(moved)
    cols = lax.broadcasted_iota(jnp.int32, (n, col_count), 1)
    spread = jnp.where(cols == col_ref[...], 1.0, 0.0).astype(jnp.bfloat16)
    out_ref[...] = mm(m_high, spread, ((1,), (0,))) + mm(m_low, spread, ((1,), (0,)))


def reorder(sub_block, target, row_ranks, col_count):
    n = sub_block.shape[0]
    spec = pl.BlockSpec(memory_space=pltpu.VMEM)
    rows = len(row_ranks) * SEP
    return pl.pallas_call(
        lambda *refs: reorder_kernel(row_ranks, col_count, *refs),
        out_shape=jax.ShapeDtypeStruct((rows, col_count), jnp.float32),
        in_specs=[spec, spec, spec],
        out_specs=spec,
        compiler_params=pltpu.CompilerParams(vmem_limit_bytes=40 << 20),
        cost_estimate=pl.CostEstimate(
            flops=4 * rows * n * (n + col_count), bytes_accessed=4 * n * n, transcendentals=0
        ),
    )(sub_block, target.reshape(1, n), target.reshape(n, 1))


def partner(block, axis, stride):
    count = lax.axis_size(axis)
    route = []
    for low in range(count):
        high = low | 1 << stride
        if high != low and high < count:
            route += [(low, high), (high, low)]
    return lax.ppermute(block, axis, route)


def after(value, *others):
    return lax.optimization_barrier((value, *others))[0]


def high_dot(a, b, dims):
    return lax.dot_general(
        a, b, (dims, ((), ())), precision=lax.Precision.HIGH, preferred_element_type=jnp.float32
    )


def new_targets(slots, left_side, upper_side):
    edge_index = slots // SEP
    west_pos = jnp.where(left_side, 1, 0).astype(jnp.int32)
    north_pos = jnp.where(upper_side, 2, 3).astype(jnp.int32)
    new_edge = jnp.where(
        edge_index == 0,
        west_pos,
        jnp.where(
            edge_index == 1, 1 - west_pos, jnp.where(edge_index == 2, north_pos, 5 - north_pos)
        ),
    )
    return new_edge * SEP + slots % SEP


def body(local_schur, boundary_map, order_first, order_second):
    row_count = lax.axis_size("gx")
    col_count = lax.axis_size("gy")
    row_bit = row_count.bit_length() - 2
    col_bit = col_count.bit_length() - 2
    pair_rows = row_count // 2
    pair_cols = col_count // 2
    row_index = lax.axis_index("gx")
    col_index = lax.axis_index("gy")
    upper = row_index < pair_rows
    left = col_index < pair_cols
    row_high = row_index // pair_rows
    col_high = col_index // pair_cols
    own_slot = 2 * col_high + row_high
    pair_row = row_index % pair_rows
    pair_col = col_index % pair_cols

    def row_swap(block):
        return partner(block, "gx", row_bit)

    def col_swap(block):
        return partner(block, "gy", col_bit)

    target = new_targets(boundary_map[0, 0], left, upper)
    first = reorder(local_schur, target, (0, 3), 4 * SEP)
    corner = first[:SEP, :SEP]
    shared = first[SEP:, 3 * SEP :]
    coupling = first[SEP:, : 3 * SEP]
    shared_other = row_swap(shared)
    corner_far = col_swap(corner)
    outer = reorder(local_schur, target, (1, 2), 3 * SEP)
    raw = outer[:, :SEP]
    keep = outer[:, SEP:]
    coupling_other = row_swap(after(coupling, shared_other))
    raw_half = col_swap(after(raw[:SEP], corner_far))
    corner_sum = corner + corner_far
    corner_other = row_swap(after(corner_sum, coupling_other))

    factor_one, inverse_one = chol(shared + shared_other, order_first[pair_row, 0])
    first_factor = jnp.where(upper, factor_one[: SEP // 2], factor_one[SEP // 2 :])
    own_panel = high_dot(coupling, inverse_one, ((0,), (1,)))
    own_inner = own_panel[:SEP]
    own_outer = own_panel[SEP:]
    inner_far = col_swap(own_inner)
    other_panel = high_dot(coupling_other, inverse_one, ((0,), (1,)))
    other_inner = other_panel[:SEP]
    other_outer = other_panel[SEP:]
    inner_far_other = row_swap(inner_far)

    keep_own = keep - high_dot(own_outer, own_outer, ((1,), (1,)))
    keep_other = -high_dot(own_outer, other_outer, ((1,), (1,)))
    base = jnp.zeros((2 * SEP, 8 * SEP), jnp.float32)
    base = lax.dynamic_update_slice(base, keep_own, (0, own_slot * 2 * SEP))
    base = lax.dynamic_update_slice(base, keep_other, (0, (own_slot ^ 1) * 2 * SEP))

    outer_far = col_swap(after(own_outer, inner_far))
    raw_rest = col_swap(after(raw[SEP:], inner_far, outer_far))
    raw_other = row_swap(after(raw, inner_far_other))

    def stack(own_part, other_part):
        return jnp.concatenate(
            [jnp.where(upper, own_part, other_part), jnp.where(upper, other_part, own_part)], axis=0
        )

    side_own = stack(own_inner, other_inner)
    side_far = stack(inner_far, inner_far_other)
    sides = jnp.concatenate([side_own, side_far], axis=1)
    zero = jnp.zeros((SEP, SEP), jnp.float32)
    corner_up = jnp.where(upper, corner_sum, corner_other)
    corner_low = jnp.where(upper, corner_other, corner_sum)
    placed = jnp.concatenate(
        [
            jnp.concatenate([corner_up, zero], axis=1),
            jnp.concatenate([zero, corner_low], axis=1),
        ],
        axis=0,
    )
    pivot_two = placed - high_dot(sides, sides, ((1,), (1,)))
    factor_two, inverse_two = chol(pivot_two, order_second[pair_row, pair_col])
    second_factor = lax.dynamic_slice(factor_two, (row_high * SEP, col_high * SEP), (SEP, SEP))

    raw_far = jnp.concatenate([raw_half, raw_rest], axis=0)
    raw_far_other = row_swap(raw_far)
    outer_far_other = row_swap(outer_far)

    inner_maps = high_dot(inverse_two, sides, ((1,), (0,)))
    map_own = -inner_maps[:, :SEP]
    map_far = -inner_maps[:, SEP:]
    half_own = jnp.where(upper, inverse_two[:, :SEP], inverse_two[:, SEP:])
    half_other = jnp.where(upper, inverse_two[:, SEP:], inverse_two[:, :SEP])

    def second(raw_part, outer_part, half, inner_map):
        return high_dot(
            jnp.concatenate([raw_part, outer_part], axis=1),
            jnp.concatenate([half, inner_map], axis=1),
            ((1,), (1,)),
        )

    second_own = second(raw, own_outer, half_own, map_own)
    local = jnp.stack(
        [
            second_own,
            second(raw_other, other_outer, half_other, map_own),
            second(raw_far, outer_far, half_own, map_far),
            second(raw_far_other, outer_far_other, half_other, map_far),
        ]
    )
    every = jnp.concatenate(
        [lax.dynamic_index_in_dim(local, slot ^ own_slot, 0, keepdims=False) for slot in range(4)],
        axis=0,
    )
    merged_schur = base - high_dot(second_own, every, ((1,), (1,)))
    return (first_factor, own_panel, second_factor, second_own, merged_schur)


def solution(mesh):
    in_specs = (P("gx", "gy"), P("gx", "gy", None), P(None, "gy", None), P())
    out_specs = (P("gx", "gy"), P("gx", "gy"), P("gx", "gy"), P("gx", "gy"), P("gx", "gy"))
    return jax.shard_map(body, mesh=mesh, in_specs=in_specs, out_specs=out_specs, check_vma=False)
```

```python
import jax
import jax.numpy as jnp
from jax import lax
from jax.experimental import pallas as pl
from jax.experimental.pallas import tpu as pltpu
from jax.sharding import PartitionSpec as P

SEP = 256

STEP = 64


def halves(x):
    high = x.astype(jnp.bfloat16)
    low = (x - high.astype(jnp.float32)).astype(jnp.bfloat16)
    return high, low


def mm(a, b, dims):
    return lax.dot_general(a, b, (dims, ((), ())), preferred_element_type=jnp.float32)


def mm3(a, b, dims):
    a_high, a_low = halves(a)
    b_high, b_low = halves(b)
    return mm(a_high, b_high, dims) + (mm(a_high, b_low, dims) + mm(a_low, b_high, dims))


def eliminate(tiles):
    count = len(tiles)
    sub = lax.broadcasted_iota(jnp.int32, (8, 128), 0)
    for t in range(count):
        cols = {
            g: [jnp.broadcast_to(tiles[g][:, 8 * t + k : 8 * t + k + 1], (8, 128)) for k in range(8)]
            for g in range(t, count)
        }
        for k in range(8):
            scale = lax.rsqrt(cols[t][k][k : k + 1, :])
            final_row = tiles[t][k : k + 1, :] * scale
            diag_row = [cols[t][m][k : k + 1, :] * scale for m in range(k + 1, 8)]
            for g in range(t, count):
                factor = cols[g][k] * scale
                if g == t:
                    factor = jnp.where(sub > k, factor, 0.0)
                for m in range(k + 1, 8):
                    cols[g][m] = cols[g][m] - factor * diag_row[m - k - 1]
                tiles[g] = tiles[g] - factor * final_row
            tiles[t] = jnp.where(sub == k, final_row, tiles[t])
    return tiles


def panels(work, n, first, last):
    lane = lax.broadcasted_iota(jnp.int32, (STEP, 128), 1)
    eye = jnp.where(
        lane == lax.broadcasted_iota(jnp.int32, (STEP, 128), 0) + STEP, 1.0, 0.0
    )

    def corner(p):
        base = p // 2 * 128
        block = work[p * STEP : (p + 1) * STEP, base : base + 128]
        if p % 2:
            block = pltpu.roll(block, STEP, 1)
        return jnp.where(lane < STEP, block, eye)

    for p in range(first, last):
        start = p * STEP
        base = start // 128 * 128
        block = corner(p)
        tiles = eliminate([block[8 * g : 8 * g + 8, :] for g in range(STEP // 8)])
        inverse = jnp.concatenate(tiles, axis=0)[:, STEP:]
        strip = mm3(inverse, work[start : start + STEP, base:], ((1,), (0,)))
        work[start : start + STEP, base:] = strip
        if start + STEP == n:
            break
        s_high, s_low = halves(strip)
        low = (start + STEP) // 128 * 128
        skip = low - base
        c_high, c_low = s_high[:, skip : n - base], s_low[:, skip : n - base]
        left = jnp.concatenate([c_high, c_high, c_low, c_low], axis=0)
        right = jnp.concatenate([s_high, s_low, s_high, s_low], axis=0)[:, skip:]
        edge = start + STEP - low
        cuts = [edge, edge + STEP, n - low]
        for begin, end in zip(cuts, cuts[1:]):
            if begin < end:
                if begin % 128 or end % 128:
                    wide = mm(left[:, begin // 128 * 128 : -(-end // 128) * 128], right, ((0,), (0,)))
                    delta = wide[begin % 128 : begin % 128 + end - begin]
                else:
                    delta = mm(left[:, begin:end], right, ((0,), (0,)))
                work[low + begin : low + end, low:] -= delta


def load_pivot(q_ref, order_ref, work):
    n = q_ref.shape[0]
    pick = (order_ref[...] == lax.broadcasted_iota(jnp.int32, (n, n), 1)).astype(jnp.float32)
    pick16 = pick.astype(jnp.bfloat16)
    q_high, q_low = halves(q_ref[...])
    rows = mm(pick16, q_high, ((1,), (0,))) + mm(pick16, q_low, ((1,), (0,)))
    r_high, r_low = halves(rows)
    work[:, :n] = mm(r_high, pick16, ((1,), (1,))) + mm(r_low, pick16, ((1,), (1,)))
    work[:, n:] = pick


def lower_of(upper):
    row = lax.broadcasted_iota(jnp.int32, upper.shape, 0)
    col = lax.broadcasted_iota(jnp.int32, upper.shape, 1)
    return jnp.where(row <= col, upper, 0.0).T


def chol_kernel(q_ref, order_ref, lower_ref, inv_ref, work):
    n = q_ref.shape[0]
    load_pivot(q_ref, order_ref, work)
    panels(work, n, 0, n // STEP)
    lower_ref[...] = lower_of(work[:, :n])
    inv_ref[...] = work[:, n:]


VM = pl.BlockSpec(memory_space=pltpu.VMEM)
PARAMS = pltpu.CompilerParams(vmem_limit_bytes=40 << 20)


def square(rows, cols):
    return jax.ShapeDtypeStruct((rows, cols), jnp.float32)


def cost(flops):
    return pl.CostEstimate(flops=flops, bytes_accessed=4 << 20, transcendentals=0)


def chol(q, order):
    n = q.shape[0]
    return pl.pallas_call(
        chol_kernel,
        out_shape=(square(n, n),) * 2,
        in_specs=[VM, VM],
        out_specs=(VM, VM),
        scratch_shapes=[pltpu.VMEM((n, 2 * n), jnp.float32)],
        compiler_params=PARAMS,
        cost_estimate=cost(n * 40_000_000),
    )(q, order.reshape(n, 1))


def reorder_kernel(row_ranks, pieces, a_ref, row_ref, col_ref, *refs):
    outs, moved = refs[:-1], refs[-1]
    step = pl.program_id(0)
    block = a_ref.shape[0]
    n = a_ref.shape[1]
    rows = lax.broadcasted_iota(jnp.int32, (SEP, block), 0)
    picked = [jnp.where(rows + rank * SEP == row_ref[...], 1.0, 0.0) for rank in row_ranks]
    pick = jnp.concatenate(picked, axis=0).astype(jnp.bfloat16)
    a_high, a_low = halves(a_ref[...])
    part = mm(pick, a_high, ((1,), (0,))) + mm(pick, a_low, ((1,), (0,)))

    @pl.when(step == 0)
    def _():
        moved[...] = part

    @pl.when(step > 0)
    def _():
        moved[...] += part

    @pl.when(step == pl.num_programs(0) - 1)
    def _():
        for (top, rows_out, left, cols_out), out_ref in zip(pieces, outs):
            m_high, m_low = halves(moved[top : top + rows_out, :])
            cols = lax.broadcasted_iota(jnp.int32, (n, cols_out), 1) + left
            spread = jnp.where(cols == col_ref[...], 1.0, 0.0).astype(jnp.bfloat16)
            out_ref[...] = mm(m_high, spread, ((1,), (0,))) + mm(m_low, spread, ((1,), (0,)))


def reorder(sub_block, row, col, row_ranks, pieces):
    n = sub_block.shape[0]
    rows = len(row_ranks) * SEP
    shapes = [(piece[1], piece[3]) for piece in pieces]
    return pl.pallas_call(
        lambda *refs: reorder_kernel(row_ranks, pieces, *refs),
        grid=(n // SEP,),
        out_shape=[square(*shape) for shape in shapes],
        in_specs=[
            pl.BlockSpec((SEP, n), lambda i: (i, 0)),
            pl.BlockSpec((1, SEP), lambda i: (0, i)),
            pl.BlockSpec((n, 1), lambda i: (0, 0)),
        ],
        out_specs=[pl.BlockSpec(shape, lambda i: (0, 0)) for shape in shapes],
        scratch_shapes=[pltpu.VMEM((rows, n), jnp.float32)],
        compiler_params=PARAMS,
        cost_estimate=cost(5_000_000_000),
    )(sub_block, row, col)


def partner(block, axis, stride):
    count = lax.axis_size(axis)
    route = []
    for low in range(count):
        high = low | 1 << stride
        if high != low and high < count:
            route += [(low, high), (high, low)]
    return lax.ppermute(block, axis, route)


def after(value, *others):
    return lax.optimization_barrier((value, *others))[0]


def high_dot(a, b, dims):
    return lax.dot_general(
        a, b, (dims, ((), ())), precision=lax.Precision.HIGH, preferred_element_type=jnp.float32
    )


def new_targets(slots, left_side, upper_side):
    edge_index = slots // SEP
    west_pos = jnp.where(left_side, 1, 0).astype(jnp.int32)
    north_pos = jnp.where(upper_side, 2, 3).astype(jnp.int32)
    new_edge = jnp.where(
        edge_index == 0,
        west_pos,
        jnp.where(
            edge_index == 1, 1 - west_pos, jnp.where(edge_index == 2, north_pos, 5 - north_pos)
        ),
    )
    return new_edge * SEP + slots % SEP


def body(local_schur, boundary_map, order_first, order_second):
    row_count = lax.axis_size("gx")
    col_count = lax.axis_size("gy")
    row_bit = row_count.bit_length() - 2
    col_bit = col_count.bit_length() - 2
    pair_rows = row_count // 2
    pair_cols = col_count // 2
    row_index = lax.axis_index("gx")
    col_index = lax.axis_index("gy")
    upper = row_index < pair_rows
    left = col_index < pair_cols
    row_high = row_index // pair_rows
    col_high = col_index // pair_cols
    own_slot = 2 * col_high + row_high
    pair_row = row_index % pair_rows
    pair_col = col_index % pair_cols

    def row_swap(block):
        return partner(block, "gx", row_bit)

    def col_swap(block):
        return partner(block, "gy", col_bit)

    target = new_targets(boundary_map[0, 0], left, upper)
    row = target.reshape(1, 4 * SEP)
    col = target.reshape(4 * SEP, 1)
    corner, coupling, shared = reorder(
        local_schur,
        row,
        col,
        (0, 3),
        ((0, SEP, 0, SEP), (SEP, SEP, 0, 3 * SEP), (SEP, SEP, 3 * SEP, SEP)),
    )
    shared_other = row_swap(shared)
    coupling_other = row_swap(coupling)
    corner_far = col_swap(corner)
    row, col, _ = lax.optimization_barrier((row, col, corner))
    raw_top, raw_low, keep = reorder(
        local_schur,
        row,
        col,
        (1, 2),
        ((0, SEP, 0, SEP), (SEP, SEP, 0, SEP), (0, 2 * SEP, SEP, 2 * SEP)),
    )
    raw_top_far = col_swap(raw_top)
    raw_top_other = row_swap(raw_top)
    raw_low_other = row_swap(raw_low)
    corner_sum = corner + corner_far
    corner_other = row_swap(corner_sum)

    factor_one, inverse_one = chol(shared + shared_other, order_first[pair_row, 0])
    first_factor = jnp.where(upper, factor_one[: SEP // 2], factor_one[SEP // 2 :])
    own_panel = high_dot(coupling, inverse_one, ((0,), (1,)))
    own_inner = own_panel[:SEP]
    own_outer = own_panel[SEP:]
    inner_far = col_swap(own_inner)
    other_panel = high_dot(coupling_other, inverse_one, ((0,), (1,)))
    other_inner = other_panel[:SEP]
    other_outer = other_panel[SEP:]
    inner_far_other = row_swap(inner_far)

    keep_own = keep - high_dot(own_outer, own_outer, ((1,), (1,)))
    keep_other = -high_dot(own_outer, other_outer, ((1,), (1,)))
    base = jnp.zeros((2 * SEP, 8 * SEP), jnp.float32)
    base = lax.dynamic_update_slice(base, keep_own, (0, own_slot * 2 * SEP))
    base = lax.dynamic_update_slice(base, keep_other, (0, (own_slot ^ 1) * 2 * SEP))

    outer_far = col_swap(after(own_outer, inner_far))
    raw_top_far_other = row_swap(after(raw_top_far, inner_far_other))

    def stack(own_part, other_part):
        return jnp.concatenate(
            [jnp.where(upper, own_part, other_part), jnp.where(upper, other_part, own_part)], axis=0
        )

    side_own = stack(own_inner, other_inner)
    side_far = stack(inner_far, inner_far_other)
    sides = jnp.concatenate([side_own, side_far], axis=1)
    zero = jnp.zeros((SEP, SEP), jnp.float32)
    corner_up = jnp.where(upper, corner_sum, corner_other)
    corner_low = jnp.where(upper, corner_other, corner_sum)
    placed = jnp.concatenate(
        [
            jnp.concatenate([corner_up, zero], axis=1),
            jnp.concatenate([zero, corner_low], axis=1),
        ],
        axis=0,
    )
    pivot_two = placed - high_dot(sides, sides, ((1,), (1,)))
    raw_low_far = col_swap(after(raw_low, inner_far))
    order_two = order_second[pair_row, pair_col]
    order_two, _ = lax.optimization_barrier((order_two, raw_top_far))
    factor_two, inverse_two = chol(pivot_two, order_two)
    outer_far_other = row_swap(outer_far)
    second_factor = lax.dynamic_slice(factor_two, (row_high * SEP, col_high * SEP), (SEP, SEP))
    raw_low_far_other = row_swap(raw_low_far)
    raw = jnp.concatenate([raw_top, raw_low], axis=0)
    raw_other = jnp.concatenate([raw_top_other, raw_low_other], axis=0)
    raw_far = jnp.concatenate([raw_top_far, raw_low_far], axis=0)
    raw_far_other = jnp.concatenate([raw_top_far_other, raw_low_far_other], axis=0)

    inner_maps = high_dot(inverse_two, sides, ((1,), (0,)))
    map_own = -inner_maps[:, :SEP]
    map_far = -inner_maps[:, SEP:]
    half_own = jnp.where(upper, inverse_two[:, :SEP], inverse_two[:, SEP:])
    half_other = jnp.where(upper, inverse_two[:, SEP:], inverse_two[:, :SEP])

    def second(raw_part, outer_part, half, inner_map):
        return high_dot(
            jnp.concatenate([raw_part, outer_part], axis=1),
            jnp.concatenate([half, inner_map], axis=1),
            ((1,), (1,)),
        )

    second_own = second(raw, own_outer, half_own, map_own)
    local = jnp.stack(
        [
            second_own,
            second(raw_other, other_outer, half_other, map_own),
            second(raw_far, outer_far, half_own, map_far),
            second(raw_far_other, outer_far_other, half_other, map_far),
        ]
    )
    every = jnp.concatenate(
        [lax.dynamic_index_in_dim(local, slot ^ own_slot, 0, keepdims=False) for slot in range(4)],
        axis=0,
    )
    merged_schur = base - high_dot(second_own, every, ((1,), (1,)))
    return (first_factor, own_panel, second_factor, second_own, merged_schur)


def solution(mesh):
    in_specs = (P("gx", "gy"), P("gx", "gy", None), P(None, "gy", None), P())
    out_specs = (P("gx", "gy"), P("gx", "gy"), P("gx", "gy"), P("gx", "gy"), P("gx", "gy"))
    return jax.shard_map(body, mesh=mesh, in_specs=in_specs, out_specs=out_specs, check_vma=False)
```

```python
import jax
import jax.numpy as jnp
from jax import lax
from jax.experimental import pallas as pl
from jax.experimental.pallas import tpu as pltpu
from jax.sharding import PartitionSpec as P

SEP = 256

STEP = 64


def halves(x):
    high = x.astype(jnp.bfloat16)
    low = (x - high.astype(jnp.float32)).astype(jnp.bfloat16)
    return high, low


def mm(a, b, dims):
    return lax.dot_general(a, b, (dims, ((), ())), preferred_element_type=jnp.float32)


def mm3(a, b, dims):
    a_high, a_low = halves(a)
    b_high, b_low = halves(b)
    return mm(a_high, b_high, dims) + (mm(a_high, b_low, dims) + mm(a_low, b_high, dims))


def eliminate(tiles):
    count = len(tiles)
    sub = lax.broadcasted_iota(jnp.int32, (8, 128), 0)
    for t in range(count):
        cols = {
            g: [jnp.broadcast_to(tiles[g][:, 8 * t + k : 8 * t + k + 1], (8, 128)) for k in range(8)]
            for g in range(t, count)
        }
        for k in range(8):
            scale = lax.rsqrt(cols[t][k][k : k + 1, :])
            final_row = tiles[t][k : k + 1, :] * scale
            diag_row = [cols[t][m][k : k + 1, :] * scale for m in range(k + 1, 8)]
            for g in range(t, count):
                factor = cols[g][k] * scale
                if g == t:
                    factor = jnp.where(sub > k, factor, 0.0)
                for m in range(k + 1, 8):
                    cols[g][m] = cols[g][m] - factor * diag_row[m - k - 1]
                tiles[g] = tiles[g] - factor * final_row
            tiles[t] = jnp.where(sub == k, final_row, tiles[t])
    return tiles


def panels(work, n, first, last):
    lane = lax.broadcasted_iota(jnp.int32, (STEP, 128), 1)
    eye = jnp.where(
        lane == lax.broadcasted_iota(jnp.int32, (STEP, 128), 0) + STEP, 1.0, 0.0
    )

    def corner(p):
        base = p // 2 * 128
        block = work[p * STEP : (p + 1) * STEP, base : base + 128]
        if p % 2:
            block = pltpu.roll(block, STEP, 1)
        return jnp.where(lane < STEP, block, eye)

    for p in range(first, last):
        start = p * STEP
        base = start // 128 * 128
        block = corner(p)
        tiles = eliminate([block[8 * g : 8 * g + 8, :] for g in range(STEP // 8)])
        inverse = jnp.concatenate(tiles, axis=0)[:, STEP:]
        strip = mm3(inverse, work[start : start + STEP, base:], ((1,), (0,)))
        work[start : start + STEP, base:] = strip
        if start + STEP == n:
            break
        s_high, s_low = halves(strip)
        low = (start + STEP) // 128 * 128
        skip = low - base
        c_high, c_low = s_high[:, skip : n - base], s_low[:, skip : n - base]
        left = jnp.concatenate([c_high, c_high, c_low, c_low], axis=0)
        right = jnp.concatenate([s_high, s_low, s_high, s_low], axis=0)[:, skip:]
        edge = start + STEP - low
        cuts = [edge, edge + STEP, n - low]
        for begin, end in zip(cuts, cuts[1:]):
            if begin < end:
                if begin % 128 or end % 128:
                    wide = mm(left[:, begin // 128 * 128 : -(-end // 128) * 128], right, ((0,), (0,)))
                    delta = wide[begin % 128 : begin % 128 + end - begin]
                else:
                    delta = mm(left[:, begin:end], right, ((0,), (0,)))
                work[low + begin : low + end, low:] -= delta


def panel_loop(work, n):
    lane = lax.broadcasted_iota(jnp.int32, (STEP, 128), 1)
    eye = jnp.where(
        lane == lax.broadcasted_iota(jnp.int32, (STEP, 128), 0) + STEP, 1.0, 0.0
    )

    def panel(p, carry):
        start = pl.multiple_of(p * STEP, STEP)
        base = pl.multiple_of((p // 2) * 128, 128)
        block = work[pl.ds(start, STEP), pl.ds(base, 128)]
        block = jnp.where(p % 2 == 0, block, pltpu.roll(block, STEP, 1))
        block = jnp.where(lane < STEP, block, eye)
        tiles = eliminate([block[8 * g : 8 * g + 8, :] for g in range(STEP // 8)])
        inverse = jnp.concatenate(tiles, axis=0)[:, STEP:]
        strip = mm3(inverse, work[pl.ds(start, STEP), :], ((1,), (0,)))
        work[pl.ds(start, STEP), :] = strip
        s_high, s_low = halves(strip)
        column = lax.broadcasted_iota(jnp.int32, (STEP, n), 1)
        c_high, c_low = halves(jnp.where(column >= start + STEP, strip[:, :n], 0.0))
        left = jnp.concatenate([c_high, c_high, c_low, c_low], axis=0)
        right = jnp.concatenate([s_high, s_low, s_high, s_low], axis=0)
        work[...] -= mm(left, right, ((0,), (0,)))
        return carry

    lax.fori_loop(0, n // STEP, panel, 0)


def load_pivot(q_ref, order_ref, work):
    n = q_ref.shape[0]
    pick = (order_ref[...] == lax.broadcasted_iota(jnp.int32, (n, n), 1)).astype(jnp.float32)
    pick16 = pick.astype(jnp.bfloat16)
    q_high, q_low = halves(q_ref[...])
    rows = mm(pick16, q_high, ((1,), (0,))) + mm(pick16, q_low, ((1,), (0,)))
    r_high, r_low = halves(rows)
    work[:, :n] = mm(r_high, pick16, ((1,), (1,))) + mm(r_low, pick16, ((1,), (1,)))
    work[:, n:] = pick


def lower_of(upper):
    row = lax.broadcasted_iota(jnp.int32, upper.shape, 0)
    col = lax.broadcasted_iota(jnp.int32, upper.shape, 1)
    return jnp.where(row <= col, upper, 0.0).T


def chol_kernel(q_ref, order_ref, lower_ref, inv_ref, work):
    n = q_ref.shape[0]
    load_pivot(q_ref, order_ref, work)
    if n > SEP:
        panels(work, n, 0, n // STEP)
    else:
        panel_loop(work, n)
    lower_ref[...] = lower_of(work[:, :n])
    inv_ref[...] = work[:, n:]


VM = pl.BlockSpec(memory_space=pltpu.VMEM)
PARAMS = pltpu.CompilerParams(vmem_limit_bytes=40 << 20)


def square(rows, cols):
    return jax.ShapeDtypeStruct((rows, cols), jnp.float32)


def cost(flops):
    return pl.CostEstimate(flops=flops, bytes_accessed=4 << 20, transcendentals=0)


def chol(q, order):
    n = q.shape[0]
    return pl.pallas_call(
        chol_kernel,
        out_shape=(square(n, n),) * 2,
        in_specs=[VM, VM],
        out_specs=(VM, VM),
        scratch_shapes=[pltpu.VMEM((n, 2 * n), jnp.float32)],
        compiler_params=PARAMS,
        cost_estimate=cost(n * 40_000_000),
    )(q, order.reshape(n, 1))


def reorder_kernel(row_ranks, pieces, a_ref, row_ref, col_ref, *refs):
    outs, moved = refs[:-1], refs[-1]
    n = a_ref.shape[0]
    a_high, a_low = halves(a_ref[...])
    rows = lax.broadcasted_iota(jnp.int32, (SEP, n), 0)
    first, stride = row_ranks[0], row_ranks[1] - row_ranks[0]

    def move(index, carry):
        rank = first + stride * index
        pick = jnp.where(rows + rank * SEP == row_ref[...], 1.0, 0.0).astype(jnp.bfloat16)
        moved[pl.ds(pl.multiple_of(index * SEP, SEP), SEP), :] = mm(
            pick, a_high, ((1,), (0,))
        ) + mm(pick, a_low, ((1,), (0,)))
        return carry

    lax.fori_loop(0, len(row_ranks), move, 0)
    m_high, m_low = halves(moved[...])
    for (top, rows_out, left, cols_out), out_ref in zip(pieces, outs):
        cols = lax.broadcasted_iota(jnp.int32, (n, cols_out), 1) + left
        spread = jnp.where(cols == col_ref[...], 1.0, 0.0).astype(jnp.bfloat16)
        part = slice(top, top + rows_out)
        out_ref[...] = mm(m_high[part], spread, ((1,), (0,))) + mm(
            m_low[part], spread, ((1,), (0,))
        )


def reorder(sub_block, row, col, row_ranks, pieces):
    n = sub_block.shape[0]
    shapes = [(piece[1], piece[3]) for piece in pieces]
    return pl.pallas_call(
        lambda *refs: reorder_kernel(row_ranks, pieces, *refs),
        out_shape=[square(*shape) for shape in shapes],
        in_specs=[VM, VM, VM],
        out_specs=[VM for _ in shapes],
        scratch_shapes=[pltpu.VMEM((len(row_ranks) * SEP, n), jnp.float32)],
        compiler_params=PARAMS,
        cost_estimate=cost(5_000_000_000),
    )(sub_block, row, col)


def partner(block, axis, stride):
    count = lax.axis_size(axis)
    route = []
    for low in range(count):
        high = low | 1 << stride
        if high != low and high < count:
            route += [(low, high), (high, low)]
    return lax.ppermute(block, axis, route)


def after(value, *others):
    return lax.optimization_barrier((value, *others))[0]


def high_dot(a, b, dims):
    return lax.dot_general(
        a, b, (dims, ((), ())), precision=lax.Precision.HIGH, preferred_element_type=jnp.float32
    )


def new_targets(slots, left_side, upper_side):
    edge_index = slots // SEP
    west_pos = jnp.where(left_side, 1, 0).astype(jnp.int32)
    north_pos = jnp.where(upper_side, 2, 3).astype(jnp.int32)
    new_edge = jnp.where(
        edge_index == 0,
        west_pos,
        jnp.where(
            edge_index == 1, 1 - west_pos, jnp.where(edge_index == 2, north_pos, 5 - north_pos)
        ),
    )
    return new_edge * SEP + slots % SEP


def body(local_schur, boundary_map, order_first, order_second):
    row_count = lax.axis_size("gx")
    col_count = lax.axis_size("gy")
    row_bit = row_count.bit_length() - 2
    col_bit = col_count.bit_length() - 2
    pair_rows = row_count // 2
    pair_cols = col_count // 2
    row_index = lax.axis_index("gx")
    col_index = lax.axis_index("gy")
    upper = row_index < pair_rows
    left = col_index < pair_cols
    row_high = row_index // pair_rows
    col_high = col_index // pair_cols
    own_slot = 2 * col_high + row_high
    pair_row = row_index % pair_rows
    pair_col = col_index % pair_cols

    def row_swap(block):
        return partner(block, "gx", row_bit)

    def col_swap(block):
        return partner(block, "gy", col_bit)

    target = new_targets(boundary_map[0, 0], left, upper)
    row = target.reshape(1, 4 * SEP)
    col = target.reshape(4 * SEP, 1)
    corner, coupling, shared = reorder(
        local_schur,
        row,
        col,
        (0, 3),
        ((0, SEP, 0, SEP), (SEP, SEP, 0, 3 * SEP), (SEP, SEP, 3 * SEP, SEP)),
    )
    shared_other = row_swap(shared)
    corner_far = col_swap(corner)
    row, col, _ = lax.optimization_barrier((row, col, corner))
    raw_top, raw_low, keep = reorder(
        local_schur,
        row,
        col,
        (1, 2),
        ((0, SEP, 0, SEP), (SEP, SEP, 0, SEP), (0, 2 * SEP, SEP, 2 * SEP)),
    )
    raw_top_far = col_swap(raw_top)
    raw_low_far = col_swap(raw_low)
    coupling_other = row_swap(after(coupling, raw_top))
    raw_top_other = row_swap(raw_top)
    raw_low_other = row_swap(raw_low)
    raw_top_far_other = row_swap(raw_top_far)
    raw_low_far_other = row_swap(raw_low_far)
    corner_sum = corner + corner_far
    corner_other = row_swap(corner_sum)

    factor_one, inverse_one = chol(shared + shared_other, order_first[pair_row, 0])
    first_factor = jnp.where(upper, factor_one[: SEP // 2], factor_one[SEP // 2 :])
    own_panel = high_dot(coupling, inverse_one, ((0,), (1,)))
    own_inner = own_panel[:SEP]
    own_outer = own_panel[SEP:]
    inner_far = col_swap(own_inner)
    coupling_other = after(coupling_other, inner_far)
    other_panel = high_dot(coupling_other, inverse_one, ((0,), (1,)))
    other_inner = other_panel[:SEP]
    other_outer = other_panel[SEP:]
    inner_far_other = row_swap(inner_far)

    keep_own = keep - high_dot(own_outer, own_outer, ((1,), (1,)))
    keep_other = -high_dot(own_outer, other_outer, ((1,), (1,)))
    base = jnp.zeros((2 * SEP, 8 * SEP), jnp.float32)
    base = lax.dynamic_update_slice(base, keep_own, (0, own_slot * 2 * SEP))
    base = lax.dynamic_update_slice(base, keep_other, (0, (own_slot ^ 1) * 2 * SEP))

    outer_far = col_swap(after(own_outer, inner_far))
    def stack(own_part, other_part):
        return jnp.concatenate(
            [jnp.where(upper, own_part, other_part), jnp.where(upper, other_part, own_part)], axis=0
        )

    side_own = stack(own_inner, other_inner)
    side_far = stack(inner_far, inner_far_other)
    sides = jnp.concatenate([side_own, side_far], axis=1)
    zero = jnp.zeros((SEP, SEP), jnp.float32)
    corner_up = jnp.where(upper, corner_sum, corner_other)
    corner_low = jnp.where(upper, corner_other, corner_sum)
    placed = jnp.concatenate(
        [
            jnp.concatenate([corner_up, zero], axis=1),
            jnp.concatenate([zero, corner_low], axis=1),
        ],
        axis=0,
    )
    pivot_two = placed - high_dot(sides, sides, ((1,), (1,)))
    order_two = order_second[pair_row, pair_col]
    order_two = after(order_two, raw_top_far_other, raw_low_far_other)
    factor_two, inverse_two = chol(pivot_two, order_two)
    outer_far_other = row_swap(outer_far)
    second_factor = lax.dynamic_slice(factor_two, (row_high * SEP, col_high * SEP), (SEP, SEP))
    raw = jnp.concatenate([raw_top, raw_low], axis=0)
    raw_other = jnp.concatenate([raw_top_other, raw_low_other], axis=0)
    raw_far = jnp.concatenate([raw_top_far, raw_low_far], axis=0)
    raw_far_other = jnp.concatenate([raw_top_far_other, raw_low_far_other], axis=0)

    inner_maps = high_dot(inverse_two, sides, ((1,), (0,)))
    map_own = -inner_maps[:, :SEP]
    map_far = -inner_maps[:, SEP:]
    half_own = jnp.where(upper, inverse_two[:, :SEP], inverse_two[:, SEP:])
    half_other = jnp.where(upper, inverse_two[:, SEP:], inverse_two[:, :SEP])

    def second(raw_part, outer_part, half, inner_map):
        return high_dot(
            jnp.concatenate([raw_part, outer_part], axis=1),
            jnp.concatenate([half, inner_map], axis=1),
            ((1,), (1,)),
        )

    second_own = second(raw, own_outer, half_own, map_own)
    local = jnp.stack(
        [
            second_own,
            second(raw_other, other_outer, half_other, map_own),
            second(raw_far, outer_far, half_own, map_far),
            second(raw_far_other, outer_far_other, half_other, map_far),
        ]
    )
    every = jnp.concatenate(
        [lax.dynamic_index_in_dim(local, slot ^ own_slot, 0, keepdims=False) for slot in range(4)],
        axis=0,
    )
    merged_schur = base - high_dot(second_own, every, ((1,), (1,)))
    return (first_factor, own_panel, second_factor, second_own, merged_schur)


def solution(mesh):
    in_specs = (P("gx", "gy"), P("gx", "gy", None), P(None, "gy", None), P())
    out_specs = (P("gx", "gy"), P("gx", "gy"), P("gx", "gy"), P("gx", "gy"), P("gx", "gy"))
    return jax.shard_map(body, mesh=mesh, in_specs=in_specs, out_specs=out_specs, check_vma=False)
```
